32 devices in a mesh: groups: 2 (over x), blk: 16 (over z, y, core).
Axes of the slice: x: 2, y: 2, z: 4, core: 2. Of those that a mesh axis runs over, the one named last changes fastest.
Arguments:
- queries: bfloat16 [16384, 1536], P(('groups', 'blk')), parts along dimension 0, may hold values from -8 to 8
- key_rows: bfloat16 [16384, 1536], P(('groups', 'blk')), parts along dimension 0, may hold values from -8 to 8
- value_rows: bfloat16 [16384, 1536], P(('groups', 'blk')), parts along dimension 0, may hold values from -24 to 24
- block_mask: int32 [64, 20], P('blk'), may hold values from 0 to 1, as said below
- out_weight: bfloat16 [1536, 3072], P(None, 'blk'), may hold values from -0.5 to 0.5
Outputs:
- projected: bfloat16 [16384, 3072], P(('groups', 'blk')), parts along dimension 0
The draws below stay inside these ranges and needn't reach their ends.
There are 2 independent parts, one for each index of `groups`. The reference program is written for one: setup_inputs(seed, part) draws one part's arguments, and reference() takes and returns one part's arrays. A program takes and returns all parts, laid end to end along the dimension named above; an argument that names none is the same for every part. Nothing has to cross between parts.
Inputs may be any that keep to these rules, and one draw needn't show every extreme that they name: `block_mask`: entry [b, (d + 2) * 4 + j] is 1 if query block b may attend key block j of the slab d slabs after its own in cyclic order (before it for negative d). A slab's own blocks are always admitted. For d = 2 and d = -2, the query blocks of one slab together admit exactly 2 of that slab's key blocks, in every draw.
All inputs are finite; a program needn't handle non-finite values.
Results may differ from the reference program's by a relative error of at most 0.009.
Values may be sent and summed in bfloat16 or wider, within the bound.
A program may use at most 192 MiB of HBM per device.

```python
import math
import jax
import jax.numpy as jnp
from jax import lax

HEADS = 12
HD = 128
D = 3072
TOK_DEV = 512
BLOCK = 128
RADIUS = 2
BPD = 4
WIN = 5
FAR = 2
TOKENS = 8192
NBLK = 64
N_BLK = 16


def drawn_values(key):
    return jnp.clip(jax.random.normal(key, (TOKENS, HEADS * HD), jnp.float32), -6.0, 6.0)


def draw_queries(key, part):
    result = drawn_values(jax.random.fold_in(key, 1))
    return result.astype(jnp.bfloat16)


def draw_key_rows(key, part):
    result = drawn_values(jax.random.fold_in(key, 2))
    return result.astype(jnp.bfloat16)


def draw_block_mask(key, part):
    slab_count = NBLK // BPD
    col_count = WIN * BPD
    coin_toss = jax.random.randint(jax.random.fold_in(key, 3), (NBLK, col_count), 0, 4)
    col_index = jnp.arange(col_count)
    offset = col_index // BPD - RADIUS
    inner_block = col_index % BPD
    rank_key = jax.random.randint(jax.random.fold_in(key, 4), (slab_count, col_count), 0, 1 << 20) * BPD + inner_block[None, :]
    same_side = offset[:, None] == offset[None, :]
    smaller = (rank_key[:, None, :] < rank_key[:, :, None]) & same_side[None, :, :]
    position = jnp.sum(smaller.astype(jnp.int32), axis=2)
    allowed = position < FAR
    forced = jax.random.randint(jax.random.fold_in(key, 5), (slab_count, col_count), 0, BPD)
    row_slab = jnp.arange(NBLK) // BPD
    row_pos = jnp.arange(NBLK) % BPD
    far_bit = ((coin_toss > 0) | (row_pos[:, None] == forced[row_slab])) & allowed[row_slab]
    near_bit = coin_toss >= 2
    chosen_mask = jnp.where(offset[None, :] == 0, True, jnp.where(jnp.abs(offset)[None, :] == RADIUS, far_bit, near_bit))
    return chosen_mask.astype(jnp.int32)


def level_of(key, shape, split, least, high):
    loudness, own = 1.0, jax.random.fold_in(key, 6)
    for dim, parts in split:
        draws = jnp.exp(jax.random.uniform(jax.random.fold_in(own, dim), (parts,), jnp.float32, least / len(split), high / len(split)))
        loudness = loudness * jnp.repeat(draws, shape[dim] // parts).reshape([-1 if axis == dim else 1 for axis in range(len(shape))])
    return loudness


def centred(key, dims, width, reach, cuts=(), kind=jnp.bfloat16):
    values = width * jax.random.normal(key, dims, jnp.float32)
    if cuts:
        values = values * level_of(key, dims, cuts, -0.22, 0.18)
    return jnp.clip(values, -reach, reach).astype(kind)


def setup_inputs(seed: int = 0, part: int = 0) -> dict:
    key_of = jax.random.split(jax.random.key(seed), 6)
    own_keys = jax.random.split(jax.random.fold_in(key_of[5], part), 6)
    return {
        "queries": draw_queries(jax.random.fold_in(jax.random.fold_in(key_of[5], part), 71), part),
        "key_rows": draw_key_rows(jax.random.fold_in(jax.random.fold_in(key_of[5], part), 71), part),
        "value_rows": centred(own_keys[2], (TOKENS, HEADS * HD), 4.0, 24.0, ((0, 16),)),
        "block_mask": draw_block_mask(jax.random.fold_in(key_of[5], 71), part),
        "out_weight": centred(key_of[4], (HEADS * HD, D), HD ** -0.5, 0.5, ((1, 16),)),
    }


neg_large = -1e+30

def one_slab(slab, queries, key_rows, value_rows, block_mask, out_weight):
    feat_width = HEADS * HD
    first_row = (slab * TOK_DEV).astype(jnp.int32)
    query_heads = lax.dynamic_slice_in_dim(queries, first_row, TOK_DEV, 0).astype(jnp.float32).reshape(TOK_DEV, HEADS, HD)
    key_parts = []
    value_parts = []
    for offset in range(-RADIUS, RADIUS + 1):
        source = ((slab + offset) % N_BLK * TOK_DEV).astype(jnp.int32)
        key_parts.append(lax.dynamic_slice_in_dim(key_rows, source, TOK_DEV, 0))
        value_parts.append(lax.dynamic_slice_in_dim(value_rows, source, TOK_DEV, 0))
    key_heads = jnp.concatenate(key_parts, axis=0).astype(jnp.float32).reshape(WIN * TOK_DEV, HEADS, HD)
    value_heads = jnp.concatenate(value_parts, axis=0).astype(jnp.float32).reshape(WIN * TOK_DEV, HEADS, HD)
    mask_rows = lax.dynamic_slice_in_dim(block_mask, (slab * BPD).astype(jnp.int32), BPD, 0)
    keeping = (mask_rows > 0)[None, :, None, :, None]
    scores = jnp.einsum('qhe,khe->hqk', query_heads, key_heads, precision=lax.Precision.HIGHEST) * (1.0 / math.sqrt(HD))
    shaped = jnp.where(keeping, scores.reshape(HEADS, BPD, BLOCK, WIN * BPD, BLOCK), neg_large)
    top_score = lax.optimization_barrier(jnp.max(shaped, axis=(3, 4), keepdims=True))
    weights = jnp.where(keeping, jnp.exp(shaped - top_score), 0.0)
    total = lax.optimization_barrier(jnp.sum(weights, axis=(3, 4))).reshape(HEADS, TOK_DEV)
    rounded = lax.optimization_barrier(weights.reshape(HEADS, TOK_DEV, WIN * TOK_DEV).astype(jnp.bfloat16))
    summed = jnp.einsum('hqk,khe->qhe', rounded.astype(jnp.float32), value_heads, precision=lax.Precision.HIGHEST)
    attention = (summed / jnp.transpose(total)[:, :, None]).reshape(TOK_DEV, feat_width).astype(jnp.bfloat16)
    return jnp.dot(attention, out_weight, preferred_element_type=jnp.float32).astype(jnp.bfloat16)

def reference(queries, key_rows, value_rows, block_mask, out_weight):

    def per_slab(slab):
        return one_slab(slab, queries, key_rows, value_rows, block_mask, out_weight)
    stacked = lax.map(per_slab, jnp.arange(N_BLK, dtype=jnp.int32))
    return stacked.reshape(TOKENS, D)
```

```python
import functools
import math

import jax
import jax.numpy as jnp
from jax import lax
from jax.experimental import pallas as pl
from jax.experimental.pallas import tpu as pltpu
from jax.sharding import PartitionSpec as P

HEADS = 12
BLOCK = 128
RADIUS = 2
NEG = -1e30
OWN, ACROSS, ALONG, SIBLING, RELAYED = range(5)


def nt_dot(a, b):
    return lax.dot_general(a, b, (((1,), (1,)), ((), ())), preferred_element_type=jnp.float32)


def attend_kernel(
    slabs, q_hbm, k_hbm, v_hbm, bias_ref, out_ref,
    q_buf, kv_buf, score_buf, send_sem, recv_sem, load_sem,
):
    tok, feat = q_hbm.shape
    head = feat // HEADS
    rows = min(256, tok)
    blocks = rows // BLOCK
    factor = math.log2(math.e) / math.sqrt(head)
    s = lax.axis_index("blk")
    c = lax.rem(s, 2)
    y = lax.rem(s // 2, 2)
    sibling = s + 1 - 2 * c
    across = s + 2 - 4 * y
    along_to = lax.rem(s + 4 - 8 * y + slabs, slabs)
    along_from = lax.rem(s - 4 + 8 * y + slabs, slabs)
    late = lax.rem(y + c, 2)

    def cols(h):
        return pl.ds(pl.multiple_of(h * head, head), head)

    def load(h, which):
        src = (k_hbm, v_hbm, q_hbm)[which]
        dst = q_buf.at[h] if which == 2 else kv_buf.at[OWN, which, h]
        return pltpu.make_async_copy(src.at[:, cols(h)], dst, load_sem.at[h, which])

    def send(kind, h, which, source, target):
        return pltpu.make_async_remote_copy(
            src_ref=source,
            dst_ref=kv_buf.at[kind, which, h],
            send_sem=send_sem.at[kind - 1, h, which],
            recv_sem=recv_sem.at[kind - 1, h, which],
            device_id={"blk": target},
            device_id_type=pl.DeviceIdType.MESH,
        )

    def own_send(kind, h, which, target):
        return send(kind, h, which, (k_hbm, v_hbm)[which].at[:, cols(h)], target)

    def pass_on(kind, held, h, which, target):
        return send(kind, h, which, kv_buf.at[held, which, h], target)

    def arrived(kind, h):
        for which in range(2):
            own_send(kind, h, which, sibling).wait_recv()

    barrier = pltpu.get_barrier_semaphore()
    for device in (sibling, across, along_to, along_from):
        pl.semaphore_signal(
            barrier, inc=1, device_id={"blk": device}, device_id_type=pl.DeviceIdType.MESH
        )
    pl.semaphore_wait(barrier, 4)

    def begin(h, carry):
        for which in range(2):
            own_send(ACROSS, h, which, across).start()
        for which in range(2):
            own_send(SIBLING, h, which, sibling).start()
        for which in range(3):
            load(h, which).start()
        return carry

    lax.fori_loop(0, HEADS, begin, 0)

    def head_rows(h, part):
        first = pl.multiple_of(part * rows, rows)
        q = q_buf[h, pl.ds(first, rows), :]
        peak = jnp.full((rows, 128), NEG, jnp.float32)
        for j in range(5):
            raw = nt_dot(q, kv_buf[j, 0, h]) * factor
            for b in range(blocks):
                for n in range(tok // BLOCK):
                    col = j * tok + n * BLOCK
                    piece = raw[b * BLOCK : (b + 1) * BLOCK, n * BLOCK : (n + 1) * BLOCK]
                    piece = piece + bias_ref[part * blocks + b, :, col : col + BLOCK]
                    score_buf[b * BLOCK : (b + 1) * BLOCK, col : col + BLOCK] = piece
            for n in range(tok // BLOCK):
                col = j * tok + n * BLOCK
                peak = jnp.maximum(peak, score_buf[:, col : col + BLOCK])
        top = jnp.max(peak, axis=1, keepdims=True)
        mass = jnp.zeros((rows, 128), jnp.float32)
        total = jnp.zeros((rows, head), jnp.float32)
        for j in range(5):
            weights = jnp.exp2(score_buf[:, j * tok : (j + 1) * tok] - top)
            for n in range(tok // BLOCK):
                mass = mass + weights[:, n * BLOCK : (n + 1) * BLOCK]
            total = total + jnp.dot(
                weights.astype(jnp.bfloat16), kv_buf[j, 1, h], preferred_element_type=jnp.float32
            )
        result = total / jnp.sum(mass, axis=1, keepdims=True)
        out_ref[pl.ds(first, rows), cols(h)] = result.astype(out_ref.dtype)

    def step(i, carry):
        @pl.when(i < HEADS)
        def _():
            arrived(ACROSS, i)
            for which in range(2):
                pass_on(ALONG, ACROSS, i, which, along_to).start()

            @pl.when(late == 0)
            def _():
                for which in range(2):
                    pass_on(RELAYED, ACROSS, i, which, sibling).start()

        @pl.when((i >= 1) & (i < HEADS + 1) & (late == 1))
        def _():
            h = i - 1
            arrived(ALONG, h)
            for which in range(2):
                pass_on(RELAYED, ALONG, h, which, sibling).start()

        @pl.when(i >= 2)
        def _():
            h = i - 2
            for which in range(3):
                load(h, which).wait()
            arrived(SIBLING, h)

            @pl.when(late == 0)
            def _():
                arrived(ALONG, h)

            arrived(RELAYED, h)

            def part_step(part, carry):
                head_rows(h, part)
                return carry

            lax.fori_loop(0, tok // rows, part_step, 0)

        return carry

    lax.fori_loop(0, HEADS + 2, step, 0)

    def finish(h, carry):
        for kind in (ACROSS, ALONG, SIBLING, RELAYED):
            for which in range(2):
                own_send(kind, h, which, sibling).wait_send()
        return carry

    lax.fori_loop(0, HEADS, finish, 0)


def attend(slabs, queries, key_rows, value_rows, bias):
    tok, feat = queries.shape
    head = feat // HEADS
    return pl.pallas_call(
        functools.partial(attend_kernel, slabs),
        out_shape=jax.ShapeDtypeStruct((tok, feat), jnp.bfloat16),
        in_specs=[pl.BlockSpec(memory_space=pl.ANY)] * 3
        + [pl.BlockSpec(memory_space=pltpu.VMEM)],
        out_specs=pl.BlockSpec(memory_space=pltpu.VMEM),
        scratch_shapes=[
            pltpu.VMEM((HEADS, tok, head), jnp.bfloat16),
            pltpu.VMEM((5, 2, HEADS, tok, head), jnp.bfloat16),
            pltpu.VMEM((min(256, tok), 5 * tok), jnp.float32),
            pltpu.SemaphoreType.DMA((4, HEADS, 2)),
            pltpu.SemaphoreType.DMA((4, HEADS, 2)),
            pltpu.SemaphoreType.DMA((HEADS, 3)),
        ],
        compiler_params=pltpu.CompilerParams(
            collective_id=0, has_side_effects=True, vmem_limit_bytes=60 * 2**20
        ),
    )(queries, key_rows, value_rows, bias)


def local(slabs, queries, key_rows, value_rows, block_mask, out_weight):
    s = lax.axis_index("blk")
    c = s % 2
    y = (s // 2) % 2
    per_slab = queries.shape[0] // BLOCK
    table = jnp.where(block_mask > 0, 0.0, NEG).astype(jnp.float32)
    table = table.reshape(block_mask.shape[0], 2 * RADIUS + 1, per_slab)
    back2, back1, own, next1, next2 = (table[:, d] for d in range(5))
    ordered = jnp.concatenate(
        (
            own,
            jnp.where(y == 0, next2, back2),
            jnp.where(y == 0, back2, next2),
            jnp.where(c == 0, next1, back1),
            jnp.where(c == 0, back1, next1),
        ),
        axis=1,
    )
    bias = jnp.repeat(ordered, BLOCK, axis=1)[:, None, :]
    attention = attend(slabs, queries, key_rows, value_rows, bias)
    weight = lax.all_gather(out_weight, "blk", axis=1, tiled=True)
    return jnp.dot(attention, weight, preferred_element_type=jnp.float32).astype(jnp.bfloat16)


def solution(mesh):
    in_specs = (
        P(("groups", "blk"), None),
        P(("groups", "blk"), None),
        P(("groups", "blk"), None),
        P("blk", None),
        P(None, "blk"),
    )
    out_specs = P(("groups", "blk"), None)
    body = functools.partial(local, mesh.shape["blk"])
    return jax.shard_map(body, mesh=mesh, in_specs=in_specs, out_specs=out_specs, check_vma=False)
```

```python
import functools
import math

import jax
import jax.numpy as jnp
from jax import lax
from jax.experimental import pallas as pl
from jax.experimental.pallas import tpu as pltpu
from jax.sharding import PartitionSpec as P

HEADS = 12
BLOCK = 128
RADIUS = 2
NEG = -1e30
OWN, ACROSS, ALONG, SIBLING, RELAYED = range(5)


def nt_dot(a, b):
    return lax.dot_general(a, b, (((1,), (1,)), ((), ())), preferred_element_type=jnp.float32)


LOOKAHEAD = 4
EARLY = 8


def attend_kernel(slabs, project, *refs):
    if project:
        q_hbm, k_hbm, v_hbm, bias_ref, w_hbm, out_ref = refs[:6]
        q_buf, kv_buf, score_buf, send_sem, recv_sem, load_sem = refs[6:12]
        heads_ref, w_buf, sum_buf, w_send, w_recv, w_load = refs[12:]
    else:
        q_hbm, k_hbm, v_hbm, bias_ref, heads_ref = refs[:5]
        q_buf, kv_buf, score_buf, send_sem, recv_sem, load_sem = refs[5:]
    tok, feat = q_hbm.shape
    head = feat // HEADS
    rows = min(256, tok)
    blocks = rows // BLOCK
    factor = math.log2(math.e) / math.sqrt(head)
    quads = slabs // 4
    s = lax.axis_index("blk")
    g = lax.axis_index("groups")
    c = lax.rem(s, 2)
    y = lax.rem(s // 2, 2)
    sibling = s + 1 - 2 * c
    across = s + 2 - 4 * y
    along_to = lax.rem(s + 4 - 8 * y + slabs, slabs)
    along_from = lax.rem(s - 4 + 8 * y + slabs, slabs)
    late = lax.rem(y + c, 2)

    def cols(h):
        return pl.ds(pl.multiple_of(h * head, head), head)

    def load(h, which):
        src = (k_hbm, v_hbm, q_hbm)[which]
        dst = q_buf.at[h] if which == 2 else kv_buf.at[OWN, which, h]
        return pltpu.make_async_copy(src.at[:, cols(h)], dst, load_sem.at[h, which])

    def send(kind, h, which, source, target):
        return pltpu.make_async_remote_copy(
            src_ref=source,
            dst_ref=kv_buf.at[kind, which, h],
            send_sem=send_sem.at[kind - 1, h, which],
            recv_sem=recv_sem.at[kind - 1, h, which],
            device_id={"blk": target},
            device_id_type=pl.DeviceIdType.MESH,
        )

    def own_send(kind, h, which, target):
        return send(kind, h, which, (k_hbm, v_hbm)[which].at[:, cols(h)], target)

    def pass_on(kind, held, h, which, target):
        return send(kind, h, which, kv_buf.at[held, which, h], target)

    def arrived(kind, h):
        for which in range(2):
            own_send(kind, h, which, sibling).wait_recv()

    if project:
        width = w_hbm.shape[0]
        half = width // 2
        far_sibling = across + 1 - 2 * c

        def slot(base, k):
            return lax.rem(base - 4 * k + slabs, slabs)

        def w_rows(index, part):
            if part is None:
                return pl.ds(pl.multiple_of(index * width, 32), width)
            return pl.ds(pl.multiple_of(index * width + part * half, 32), half)

        def w_copy(sem, k, index, part, target, own=False):
            place = w_buf.at[w_rows(index, part)]
            if not own:
                source = place
            elif part is None:
                source = w_hbm
            else:
                source = w_hbm.at[pl.ds(pl.multiple_of(part * half, 32), half)]
            return pltpu.make_async_remote_copy(
                src_ref=source,
                dst_ref=place,
                send_sem=w_send.at[sem, k],
                recv_sem=w_recv.at[sem, k],
                device_id=target,
                device_id_type=pl.DeviceIdType.MESH,
            )

        def w_along(k, index, target):
            return w_copy(0, k, index, g, {"blk": target}, own=True)

        def w_across(k, index, own=False):
            return w_copy(1, k, index, g, {"blk": across}, own=own)

        def w_twin(near, k, index, part):
            return w_copy(2 + near, k, index, part, {"groups": 1 - g})

        def w_sibling(near, k, index, own=False):
            return w_copy(4 + near, k, index, None, {"blk": sibling}, own=own)

        w_keep = pltpu.make_async_copy(w_hbm, w_buf.at[w_rows(s, None)], w_load.at[0])

    barrier = pltpu.get_barrier_semaphore()
    if project:
        peers = [{"blk": sibling}, {"blk": across}, {"groups": 1 - g}]
        peers += [{"blk": lax.rem(s + 4 * k, slabs)} for k in range(1, quads)]
    else:
        peers = [{"blk": device} for device in (sibling, across, along_to, along_from)]
    for device in peers:
        pl.semaphore_signal(
            barrier, inc=1, device_id=device, device_id_type=pl.DeviceIdType.MESH
        )
    pl.semaphore_wait(barrier, len(peers))

    def begin_across(h, carry):
        for which in range(2):
            own_send(ACROSS, h, which, across).start()
        return carry

    def begin(h, carry):
        for which in range(2):
            own_send(SIBLING, h, which, sibling).start()
        for which in range(3):
            load(h, which).start()
        return carry

    if project:
        lax.fori_loop(0, 2, begin_across, 0)
        for k in range(1, quads):
            w_along(k, s, lax.rem(s + 4 * k, slabs)).start()
        w_across(0, s, own=True).start()
        lax.fori_loop(2, LOOKAHEAD, begin_across, 0)
        lax.fori_loop(0, HEADS, begin, 0)
        w_keep.start()
        w_sibling(1, 0, s, own=True).start()
    else:
        lax.fori_loop(0, LOOKAHEAD, begin_across, 0)
        lax.fori_loop(0, HEADS, begin, 0)

    def head_rows(h, part):
        first = pl.multiple_of(part * rows, rows)
        q = q_buf[h, pl.ds(first, rows), :]
        peak = jnp.full((rows, 128), NEG, jnp.float32)
        for j in range(5):
            raw = nt_dot(q, kv_buf[j, 0, h]) * factor
            for b in range(blocks):
                for n in range(tok // BLOCK):
                    col = j * tok + n * BLOCK
                    piece = raw[b * BLOCK : (b + 1) * BLOCK, n * BLOCK : (n + 1) * BLOCK]
                    piece = piece + bias_ref[part * blocks + b, :, col : col + BLOCK]
                    score_buf[b * BLOCK : (b + 1) * BLOCK, col : col + BLOCK] = piece
            for n in range(tok // BLOCK):
                col = j * tok + n * BLOCK
                peak = jnp.maximum(peak, score_buf[:, col : col + BLOCK])
        top = jnp.max(peak, axis=1, keepdims=True)
        mass = jnp.zeros((rows, 128), jnp.float32)
        total = jnp.zeros((rows, head), jnp.float32)
        for j in range(5):
            weights = jnp.exp2(score_buf[:, j * tok : (j + 1) * tok] - top)
            for n in range(tok // BLOCK):
                mass = mass + weights[:, n * BLOCK : (n + 1) * BLOCK]
            total = total + jnp.dot(
                weights.astype(jnp.bfloat16), kv_buf[j, 1, h], preferred_element_type=jnp.float32
            )
        result = total / jnp.sum(mass, axis=1, keepdims=True)
        heads_ref[pl.ds(first, rows), cols(h)] = result.astype(jnp.bfloat16)

    def weight_step(i):
        @pl.when((i >= 1) & (i < quads))
        def _():
            index = slot(s, i)
            w_along(i, index, sibling).wait_recv()
            w_across(i, index).start()
            w_twin(1, i, index, g).start()

        @pl.when((i >= 2) & (i < quads + 2))
        def _():
            k = i - 2
            index = slot(across, k)
            w_across(k, index).wait_recv()
            w_twin(0, k, index, g).start()

        @pl.when((i >= 4) & (i < quads + 3))
        def _():
            k = i - 3
            index = slot(s, k)
            w_twin(1, k, index, 1 - g).wait_recv()
            w_sibling(1, k, index).start()

        @pl.when((i >= 4) & (i < quads + 4))
        def _():
            k = i - 4
            index = slot(across, k)
            w_twin(0, k, index, 1 - g).wait_recv()
            w_sibling(0, k, index).start()

    def step(i, carry):
        @pl.when(i < HEADS)
        def _():
            arrived(ACROSS, i)
            for which in range(2):
                pass_on(ALONG, ACROSS, i, which, along_to).start()

            @pl.when(late == 0)
            def _():
                for which in range(2):
                    pass_on(RELAYED, ACROSS, i, which, sibling).start()

        @pl.when(i + LOOKAHEAD < HEADS)
        def _():
            begin_across(i + LOOKAHEAD, 0)

        @pl.when((i >= 1) & (i < HEADS + 1) & (late == 1))
        def _():
            h = i - 1
            arrived(ALONG, h)
            for which in range(2):
                pass_on(RELAYED, ALONG, h, which, sibling).start()

        if project:
            weight_step(i)

        @pl.when(i >= 2)
        def _():
            h = i - 2
            for which in range(3):
                load(h, which).wait()
            arrived(SIBLING, h)

            @pl.when(late == 0)
            def _():
                arrived(ALONG, h)

            arrived(RELAYED, h)

            def part_step(part, carry):
                head_rows(h, part)
                return carry

            lax.fori_loop(0, tok // rows, part_step, 0)

        if project:

            @pl.when(i == EARLY + 2)
            def _():
                w_keep.wait()
                for k in range(quads):
                    w_sibling(1, k, slot(sibling, k)).wait_recv()
                    w_sibling(0, k, slot(far_sibling, k)).wait_recv()
                lax.fori_loop(0, w_buf.shape[0] // 512, early_tile, 0)

        return carry

    if project:
        cut = EARLY * head

        def early_tile(t, carry):
            place = pl.ds(pl.multiple_of(t * 512, 512), 512)
            sum_buf[:, place] = nt_dot(heads_ref[:, :cut], w_buf[place, :cut])
            return carry

        def last_tile(t, carry):
            place = pl.ds(pl.multiple_of(t * 512, 512), 512)
            rest = nt_dot(heads_ref[:, cut:], w_buf[place, cut:])
            out_ref[:, place] = (sum_buf[:, place] + rest).astype(out_ref.dtype)
            return carry

    lax.fori_loop(0, HEADS + 2, step, 0)
    if project:
        lax.fori_loop(0, w_buf.shape[0] // 512, last_tile, 0)

    def finish(h, carry):
        for kind in (ACROSS, ALONG, SIBLING, RELAYED):
            for which in range(2):
                own_send(kind, h, which, sibling).wait_send()
        return carry

    lax.fori_loop(0, HEADS, finish, 0)
    if project:
        for k in range(quads):
            if k:
                w_along(k, s, sibling).wait_send()
                w_twin(1, k, slot(s, k), g).wait_send()
            w_across(k, slot(s, k)).wait_send()
            w_twin(0, k, slot(across, k), g).wait_send()
            w_sibling(1, k, slot(s, k)).wait_send()
            w_sibling(0, k, slot(across, k)).wait_send()


def attend(slabs, project, queries, key_rows, value_rows, bias, weight):
    tok, feat = queries.shape
    head = feat // HEADS
    scratch = [
        pltpu.VMEM((HEADS, tok, head), jnp.bfloat16),
        pltpu.VMEM((5, 2, HEADS, tok, head), jnp.bfloat16),
        pltpu.VMEM((min(256, tok), 5 * tok), jnp.float32),
        pltpu.SemaphoreType.DMA((4, HEADS, 2)),
        pltpu.SemaphoreType.DMA((4, HEADS, 2)),
        pltpu.SemaphoreType.DMA((HEADS, 3)),
    ]
    in_specs = [pl.BlockSpec(memory_space=pl.ANY)] * 3 + [pl.BlockSpec(memory_space=pltpu.VMEM)]
    operands = [queries, key_rows, value_rows, bias]
    width = feat
    if project:
        width = slabs * weight.shape[0]
        in_specs.append(pl.BlockSpec(memory_space=pl.ANY))
        operands.append(weight)
        scratch += [
            pltpu.VMEM((tok, feat), jnp.bfloat16),
            pltpu.VMEM((width, feat), jnp.bfloat16),
            pltpu.VMEM((tok, width), jnp.float32),
            pltpu.SemaphoreType.DMA((6, slabs // 4)),
            pltpu.SemaphoreType.DMA((6, slabs // 4)),
            pltpu.SemaphoreType.DMA((1,)),
        ]
    return pl.pallas_call(
        functools.partial(attend_kernel, slabs, project),
        out_shape=jax.ShapeDtypeStruct((tok, width), jnp.bfloat16),
        in_specs=in_specs,
        out_specs=pl.BlockSpec(memory_space=pltpu.VMEM),
        scratch_shapes=scratch,
        compiler_params=pltpu.CompilerParams(
            collective_id=0, has_side_effects=True, vmem_limit_bytes=60 * 2**20
        ),
    )(*operands)


def local(slabs, groups, queries, key_rows, value_rows, block_mask, out_weight):
    s = lax.axis_index("blk")
    c = s % 2
    y = (s // 2) % 2
    per_slab = queries.shape[0] // BLOCK
    table = jnp.where(block_mask > 0, 0.0, NEG).astype(jnp.float32)
    table = table.reshape(block_mask.shape[0], 2 * RADIUS + 1, per_slab)
    back2, back1, own, next1, next2 = (table[:, d] for d in range(5))
    ordered = jnp.concatenate(
        (
            own,
            jnp.where(y == 0, next2, back2),
            jnp.where(y == 0, back2, next2),
            jnp.where(c == 0, next1, back1),
            jnp.where(c == 0, back1, next1),
        ),
        axis=1,
    )
    bias = jnp.repeat(ordered, BLOCK, axis=1)[:, None, :]
    width = out_weight.shape[1]
    project = groups == 2 and 3 <= slabs // 4 <= 4 and width % 64 == 0 and slabs * width % 512 == 0
    if project:
        return attend(slabs, True, queries, key_rows, value_rows, bias, out_weight.T)
    attention = attend(slabs, False, queries, key_rows, value_rows, bias, None)
    weight = lax.all_gather(out_weight, "blk", axis=1, tiled=True)
    return jnp.dot(attention, weight, preferred_element_type=jnp.float32).astype(jnp.bfloat16)


def solution(mesh):
    in_specs = (
        P(("groups", "blk"), None),
        P(("groups", "blk"), None),
        P(("groups", "blk"), None),
        P("blk", None),
        P(None, "blk"),
    )
    out_specs = P(("groups", "blk"), None)
    body = functools.partial(local, mesh.shape["blk"], mesh.shape["groups"])
    return jax.shard_map(body, mesh=mesh, in_specs=in_specs, out_specs=out_specs, check_vma=False)
```
